512 devices in a mesh: slab: 16 (over z, core), cross: 32 (over y, x).
Axes of the slice: x: 4, y: 8, z: 8, core: 2. Of those that a mesh axis runs over, the one named last changes fastest.
Arguments:
- thickness: int32 [16], P('slab'), may hold values from 1 to 4, as said below
- layer_sources: bfloat16 [64, 128, 32768], P('slab', None, 'cross'), may hold values from -6 to 6
- green_down: bfloat16 [16, 1536, 128, 128], P('slab', 'cross'), may hold values from -0.1875 to 0.1875
- column_down: int32 [16, 1536], P('slab', 'cross'), may hold values from 0 to 255, as said below
- green_up: bfloat16 [16, 1536, 128, 128], P('slab', 'cross'), may hold values from -0.1875 to 0.1875
- column_up: int32 [16, 1536], P('slab', 'cross'), may hold values from 0 to 255, as said below
Outputs:
- down_traces: bfloat16 [16, 128, 32768], P('slab', None, 'cross')
- up_traces: bfloat16 [16, 128, 32768], P('slab', None, 'cross')
The draws below stay inside these ranges and needn't reach their ends.
Inputs may be any that keep to these rules, and one draw needn't show every extreme that they name: `thickness`: each slab has 1 to 4 layers; some slab has exactly 4 and another exactly 1. `column_down`: the 6 columns of block row i are distinct, each equals (i + o) modulo 256 for some o with -4 <= o <= 4, and they include (i + 4) modulo 256. `column_up`: as for column_down.
All inputs are finite; a program needn't handle non-finite values.
Results may differ from the reference program's by a relative error of at most 0.015.
Values may be sent and summed in bfloat16 or wider, within the bound.
A program may use at most 64 MiB of HBM per device.

```python
import jax
import jax.numpy as jnp

TR = 32768
BS = 128
KB = 6
HB = 4
TMAX = 4
SRC = 128
NB = 256
LAYERS = 64
N_SLAB = 16


def draw_thickness(key, part):
    first = jax.random.fold_in(key, 11)
    second = jax.random.fold_in(key, 12)
    third = jax.random.fold_in(key, 13)
    values = jax.random.randint(first, (N_SLAB,), 1, TMAX + 1)
    where_max = jax.random.randint(second, (), 0, N_SLAB)
    step_min = jax.random.randint(third, (), 1, N_SLAB)
    where_min = (where_max + step_min) % N_SLAB
    slots = jnp.arange(N_SLAB)
    values = jnp.where(slots == where_min, 1, values)
    return jnp.where(slots == where_max, TMAX, values).astype(jnp.int32)


def block_columns(key):
    keys = jax.random.split(key, N_SLAB * NB)
    inner = jax.vmap(lambda one: jax.random.permutation(one, 2 * HB)[:KB - 1])(keys)
    inner = inner.astype(jnp.int32) - HB
    ends = jnp.full((N_SLAB * NB, 1), HB, jnp.int32)
    offsets = jnp.concatenate([ends, inner], axis=1)
    offsets = offsets.reshape(N_SLAB, NB, KB)
    rows = jnp.arange(NB)[None, :, None]
    return ((rows + offsets) % NB).reshape(N_SLAB, NB * KB).astype(jnp.int32)


def draw_column_down(key, part):
    return block_columns(jax.random.fold_in(key, 21))


def draw_column_up(key, part):
    return block_columns(jax.random.fold_in(key, 22))


def level_of(own_key, dims, pieces, smallest, largest):
    loudness = 1.0
    for position, parts in pieces:
        steps = jax.random.uniform(jax.random.fold_in(jax.random.fold_in(own_key, 6), position), (parts,), jnp.float32, smallest / len(pieces), largest / len(pieces))
        loudness = loudness * jnp.repeat(jnp.exp(steps), dims[position] // parts).reshape((-1,) + (1,) * (len(dims) - 1 - position))
    return loudness


def noise(rng, dims, width, bound, shards=(), held_as=jnp.bfloat16):
    result = jax.random.normal(rng, dims, jnp.float32) * width
    if len(shards) > 0:
        result = level_of(rng, dims, shards, -0.22, 0.18) * result
    return jnp.clip(result, min=-bound, max=bound).astype(held_as)


def setup_inputs(seed: int = 0) -> dict:
    splits = jax.random.split(jax.random.key(seed), 7)
    thickness = draw_thickness(jax.random.fold_in(splits[6], 71), 0)
    layer_sources = noise(splits[1], (LAYERS, SRC, TR), 1.0, 6.0, ((0, 16), (2, 32)))
    green_down = noise(splits[2], (N_SLAB, NB * KB, BS, BS), (KB * BS * 7 // 5) ** -0.5, 0.1875, ((0, 16), (1, 32)))
    column_down = draw_column_down(jax.random.fold_in(splits[6], 71), 0)
    green_up = noise(splits[4], (N_SLAB, NB * KB, BS, BS), (KB * BS * 7 // 5) ** -0.5, 0.1875, ((0, 16), (1, 32)))
    column_up = draw_column_up(jax.random.fold_in(splits[6], 71), 0)
    return dict(thickness=thickness, layer_sources=layer_sources, green_down=green_down, column_down=column_down, green_up=green_up, column_up=column_up)


def apply_green(trace, blocks, columns):
    rows = trace.shape[0]
    nblk = trace.shape[1] // blocks.shape[-1]
    bsize = blocks.shape[-1]
    tiles = trace.astype(jnp.float32).reshape(rows, nblk, bsize)
    picked = jnp.take(tiles, columns, axis=1)
    prod = jnp.einsum("snb,nab->sna", picked, blocks.astype(jnp.float32))
    kcount = blocks.shape[0] // nblk
    return prod.reshape(rows, nblk, kcount, bsize).sum(axis=2).reshape(rows, nblk * bsize)


def slab_source(layer_sources, thickness, slab_id):
    depth = layer_sources.shape[0] // thickness.shape[0]
    layers = jax.lax.dynamic_slice_in_dim(layer_sources, slab_id * depth, depth, 0).astype(jnp.float32)
    keep = (jnp.arange(depth) < thickness[slab_id]).astype(jnp.float32)
    return jnp.sum(layers * keep[:, None, None], axis=0)


def reference(thickness, layer_sources, green_down, column_down, green_up, column_up):
    slabs = thickness.shape[0]
    downs = []
    previous = None
    for slab_id in range(slabs):
        value = slab_source(layer_sources, thickness, slab_id)
        if previous is not None:
            value = value + apply_green(previous, green_down[slab_id], column_down[slab_id])
        previous = value.astype(jnp.bfloat16)
        downs.append(previous)
    ups = [None] * slabs
    previous = None
    for slab_id in range(slabs - 1, -1, -1):
        value = slab_source(layer_sources, thickness, slab_id)
        if previous is not None:
            value = value + apply_green(previous, green_up[slab_id], column_up[slab_id])
        previous = value.astype(jnp.bfloat16)
        ups[slab_id] = previous
    return jnp.stack(downs), jnp.stack(ups)
```

```python
import functools

import jax
import jax.numpy as jnp
from jax import lax
from jax.experimental import pallas as pl
from jax.experimental.pallas import tpu as pltpu
from jax.sharding import PartitionSpec as P

HB = 4
MB = 4
MESH = pl.DeviceIdType.MESH


def sweep(
    slabs, laterals, kcount,
    thick_ref, layers_hbm, gdown_hbm, cdown_ref, gup_hbm, cup_ref,
    down_hbm, up_hbm,
    layers, green, source, ext, near, out,
    layer_sem, green_sem, recv_sem, send_sem, store_sem,
):
    depth, rows_all, width = layers.shape
    groups = ext.shape[1]
    rows = ext.shape[2]
    bsize = green.shape[-1]
    per_dev = width // bsize
    halo = HB * bsize
    slab = lax.axis_index("slab")
    cross = lax.axis_index("cross")
    right = lax.rem(cross + 1, laterals)
    left = lax.rem(cross + laterals - 1, laterals)
    last = slabs - 1

    def group_rows(m):
        return pl.ds(pl.multiple_of(m * rows, rows), rows)

    def layer_copy(m):
        part = group_rows(m)
        return pltpu.make_async_copy(
            layers_hbm.at[:, part, :], layers.at[:, part, :], layer_sem.at[m]
        )

    green_copies = [
        pltpu.make_async_copy(gdown_hbm.at[0], green.at[0], green_sem.at[0]),
        pltpu.make_async_copy(gup_hbm.at[0], green.at[1], green_sem.at[1]),
    ]
    for m in range(groups):
        layer_copy(m).start()
    for copy in green_copies:
        copy.start()

    barrier = pltpu.get_barrier_semaphore()
    for step, there in ((1, slab < last), (-1, slab > 0)):
        @pl.when(there)
        def _(step=step):
            for side in (left, cross, right):
                pl.semaphore_signal(
                    barrier, inc=1,
                    device_id={"slab": slab + step, "cross": side}, device_id_type=MESH,
                )
    pl.semaphore_wait(
        barrier, 3 * ((slab < last).astype(jnp.int32) + (slab > 0).astype(jnp.int32))
    )

    def sends(d, m):
        target = slab + 1 - 2 * d
        part = group_rows(m)
        pieces = (
            (0, halo, left, halo + width),
            (width - halo, halo, right, 0),
            (0, width, cross, halo),
        )
        return [
            pltpu.make_async_remote_copy(
                src_ref=out.at[d, part, pl.ds(at, size)],
                dst_ref=ext.at[d, m, :, pl.ds(to, size)],
                send_sem=send_sem.at[d, m, i],
                recv_sem=recv_sem.at[d, m, i],
                device_id={"slab": target, "cross": side},
                device_id_type=MESH,
            )
            for i, (at, size, side, to) in enumerate(pieces)
        ]

    def has_send(d):
        return slab != last * (1 - d)

    def store(d, m, ref):
        part = group_rows(m)
        return pltpu.make_async_copy(
            out.at[d, part, :], ref.at[0, part, :], store_sem.at[d, m]
        )

    def emit(d, m):
        @pl.when(has_send(d))
        def _():
            for copy in sends(d, m):
                copy.start()

        @pl.when(d == 0)
        def _():
            store(0, m, down_hbm).start()

        @pl.when(d == 1)
        def _():
            store(1, m, up_hbm).start()

    first = jnp.where(slab < slabs // 2, 0, 1)
    edge = jnp.logical_or(slab == 0, slab == last)

    @pl.loop(0, groups)
    def _(m):
        layer_copy(m).wait()
        part = group_rows(m)
        total = None
        for k in range(depth):
            keep = (k < thick_ref[0]).astype(jnp.float32)
            term = layers[k, part, :].astype(jnp.float32) * keep
            total = term if total is None else total + term
        source[part, :] = total

        @pl.when(edge)
        def _():
            out[first, part, :] = total.astype(out.dtype)
            emit(first, m)

    for copy in green_copies:
        copy.wait()

    def column(d, n):
        raw = jnp.where(d == 0, cdown_ref[0, n], cup_ref[0, n])
        return jnp.bitwise_and(raw - cross * per_dev + HB, near.shape[0] - 1)

    @pl.loop(jnp.where(edge, groups, 0), 2 * groups)
    def _(t):
        later = t // groups
        m = t - later * groups
        d = first + later - 2 * first * later
        for copy in sends(d, m):
            copy.wait_recv()
        part = group_rows(m)
        for blk in range(per_dev + 2 * HB):
            near[blk] = ext[d, m, :, blk * bsize:(blk + 1) * bsize]
        for b in range(per_dev):
            base = b * kcount
            picked = jnp.concatenate(
                [near[column(d, base + k)] for k in range(kcount)], axis=1
            )
            weights = jnp.concatenate(
                [green[d, base + k] for k in range(kcount)], axis=1
            )
            product = lax.dot_general(
                picked, weights, (((1,), (1,)), ((), ())),
                preferred_element_type=jnp.float32,
            )
            lanes = slice(b * bsize, (b + 1) * bsize)
            out[d, part, lanes] = (product + source[part, lanes]).astype(out.dtype)
        emit(d, m)

    for d, ref in ((0, down_hbm), (1, up_hbm)):
        @pl.when(has_send(d))
        def _(d=d):
            @pl.loop(0, groups)
            def _(m):
                for copy in sends(d, m):
                    copy.wait_send()

        @pl.loop(0, groups)
        def _(m, d=d, ref=ref):
            store(d, m, ref).wait()


def shards(slabs, laterals, thickness, layer_sources, green_down, column_down, green_up, column_up):
    depth, sources, width = layer_sources.shape
    blocks, bsize = green_down.shape[1], green_down.shape[-1]
    kcount = blocks // (width // bsize)
    rows = sources // MB
    extended = width + 2 * HB * bsize
    result = jax.ShapeDtypeStruct((1, sources, width), jnp.bfloat16)
    smem = pl.BlockSpec(memory_space=pltpu.SMEM)
    anywhere = pl.BlockSpec(memory_space=pl.ANY)
    return pl.pallas_call(
        functools.partial(sweep, slabs, laterals, kcount),
        out_shape=(result, result),
        in_specs=[smem, anywhere, anywhere, smem, anywhere, smem],
        out_specs=(anywhere, anywhere),
        scratch_shapes=[
            pltpu.VMEM((depth, sources, width), jnp.bfloat16),
            pltpu.VMEM((2, blocks, bsize, bsize), jnp.bfloat16),
            pltpu.VMEM((sources, width), jnp.float32),
            pltpu.VMEM((2, MB, rows, extended), jnp.bfloat16),
            pltpu.VMEM((extended // bsize, rows, bsize), jnp.bfloat16),
            pltpu.VMEM((2, sources, width), jnp.bfloat16),
            pltpu.SemaphoreType.DMA((MB,)),
            pltpu.SemaphoreType.DMA((2,)),
            pltpu.SemaphoreType.DMA((2, MB, 3)),
            pltpu.SemaphoreType.DMA((2, MB, 3)),
            pltpu.SemaphoreType.DMA((2, MB)),
        ],
        compiler_params=pltpu.CompilerParams(collective_id=0, has_side_effects=True),
    )(thickness, layer_sources, green_down, column_down, green_up, column_up)


def solution(mesh):
    return jax.shard_map(
        functools.partial(shards, mesh.shape["slab"], mesh.shape["cross"]),
        mesh=mesh,
        in_specs=(
            P("slab"),
            P("slab", None, "cross"),
            P("slab", "cross", None, None),
            P("slab", "cross"),
            P("slab", "cross", None, None),
            P("slab", "cross"),
        ),
        out_specs=(P("slab", None, "cross"), P("slab", None, "cross")),
        check_vma=False,
    )
```

```python
import functools

import jax
import jax.numpy as jnp
from jax import lax
from jax.experimental import pallas as pl
from jax.experimental.pallas import tpu as pltpu
from jax.sharding import PartitionSpec as P

HB = 4
MB = 4
ROW = 4
MESH = pl.DeviceIdType.MESH


def sweep(
    slabs, laterals, kcount,
    thick_ref, layers_hbm, gdown_hbm, cdown_ref, gup_hbm, cup_ref,
    down_hbm, up_hbm,
    layers, green, source, ext, near, out,
    layer_sem, green_sem, recv_sem, send_sem, store_sem,
):
    depth, _, width = layers.shape
    groups, rows = ext.shape[1], ext.shape[3]
    bsize = green.shape[-1]
    per_dev = width // bsize
    half = HB * bsize
    slab = lax.axis_index("slab")
    cross = lax.axis_index("cross")
    right = lax.rem(cross + 1, laterals)
    left = lax.rem(cross + laterals - 1, laterals)
    last = slabs - 1

    def group_rows(m):
        return pl.ds(pl.multiple_of(m * rows, rows), rows)

    def layer_copy(m):
        part = group_rows(m)
        return pltpu.make_async_copy(
            layers_hbm.at[:, part, :], layers.at[:, part, :], layer_sem.at[m]
        )

    green_copies = [
        pltpu.make_async_copy(gdown_hbm.at[0], green.at[0], green_sem.at[0]),
        pltpu.make_async_copy(gup_hbm.at[0], green.at[1], green_sem.at[1]),
    ]
    for m in range(groups):
        layer_copy(m).start()
    for copy in green_copies:
        copy.start()

    barrier = pltpu.get_barrier_semaphore()
    for step, there in ((1, slab < last), (-1, slab > 0)):
        @pl.when(there)
        def _(step=step):
            for side in (left, cross, right):
                pl.semaphore_signal(
                    barrier, inc=1,
                    device_id={"slab": slab + step, "cross": side}, device_id_type=MESH,
                )
    pl.semaphore_wait(
        barrier, 3 * ((slab < last).astype(jnp.int32) + (slab > 0).astype(jnp.int32))
    )

    def remote(d, m, h, piece, side):
        return pltpu.make_async_remote_copy(
            src_ref=out.at[d, h, group_rows(m), :],
            dst_ref=ext.at[d, m, piece],
            send_sem=send_sem.at[d, m, piece],
            recv_sem=recv_sem.at[d, m, piece],
            device_id={"slab": slab + 1 - 2 * d, "cross": side},
            device_id_type=MESH,
        )

    def sends(d, m, h):
        return [
            remote(d, m, h, 3 - 3 * h, left + h * (right - left)),
            remote(d, m, h, 1 + h, cross),
        ]

    def arrived(d, m, piece):
        remote(d, m, 0, piece, cross).wait_recv()

    def has_send(d):
        return slab != last * (1 - d)

    def store(d, m, h, ref):
        return pltpu.make_async_copy(
            out.at[d, h, group_rows(m), :],
            ref.at[0, group_rows(m), h * half:(h + 1) * half],
            store_sem.at[d, m, h],
        )

    def emit(d, m, h):
        @pl.when(has_send(d))
        def _():
            for copy in sends(d, m, h):
                copy.start()

    def keep(d, m):
        for want, ref in ((0, down_hbm), (1, up_hbm)):
            @pl.when(d == want)
            def _(want=want, ref=ref):
                for h in range(2):
                    store(want, m, h, ref).start()

    first = jnp.where(slab < slabs // 2, 0, 1)
    edge = jnp.logical_or(slab == 0, slab == last)
    lead = jnp.where(lax.rem(cross, ROW) == 0, 1, 0)

    @pl.loop(0, groups)
    def _(m):
        layer_copy(m).wait()
        part = group_rows(m)
        for h in range(2):
            total = None
            for k in range(depth):
                weight = (k < thick_ref[0]).astype(jnp.float32)
                term = layers[k, part, h * half:(h + 1) * half].astype(jnp.float32) * weight
                total = term if total is None else total + term
            source[h, part, :] = total

            @pl.when(edge)
            def _():
                out[first, h, part, :] = total.astype(out.dtype)
                emit(first, m, h)

        @pl.when(edge)
        def _():
            keep(first, m)

    for copy in green_copies:
        copy.wait()

    def flip(d):
        @pl.loop(0, green.shape[1], step=2)
        def _(i):
            for j in range(2):
                green[d, i + j] = green[d, i + j].T

    early = jnp.logical_and(slab >= slabs // 4, slab < slabs - slabs // 4)

    @pl.when(jnp.logical_not(edge))
    def _():
        flip(first)

    @pl.when(jnp.logical_or(early, edge))
    def _():
        flip(1 - first)

    def column(d, n):
        raw = jnp.where(d == 0, cdown_ref[0, n], cup_ref[0, n])
        return jnp.bitwise_and(raw - cross * per_dev + HB, near.shape[0] - 1)

    def bring(d, m, piece):
        arrived(d, m, piece)
        for j in range(HB):
            near[piece * HB + j] = ext[d, m, piece, :, j * bsize:(j + 1) * bsize]

    @pl.loop(jnp.where(edge, groups, 0), 2 * groups)
    def _(t):
        later = t // groups
        m = t - later * groups
        d = first + later - 2 * first * later
        part = group_rows(m)

        @pl.when(jnp.logical_and(t == groups, jnp.logical_not(jnp.logical_or(early, edge))))
        def _():
            flip(d)

        @pl.loop(0, 2)
        def _(i):
            h = lead + i - 2 * lead * i

            @pl.when(i == 0)
            def _():
                bring(d, m, 1)
                bring(d, m, 2)
                bring(d, m, 3 * h)

            @pl.when(i == 1)
            def _():
                bring(d, m, 3 * h)

            for b in range(HB):
                base = (h * HB + b) * kcount
                picked = jnp.concatenate(
                    [near[column(d, base + k)] for k in range(kcount)], axis=1
                )
                weights = green[d, pl.ds(base, kcount)].reshape(kcount * bsize, bsize)
                product = jnp.dot(picked, weights, preferred_element_type=jnp.float32)
                lanes = slice(b * bsize, (b + 1) * bsize)
                out[d, h, part, lanes] = (product + source[h, part, lanes]).astype(out.dtype)
            emit(d, m, h)

        keep(d, m)

    for d, ref in ((0, down_hbm), (1, up_hbm)):
        @pl.when(has_send(d))
        def _(d=d):
            @pl.loop(0, groups)
            def _(m):
                for h in range(2):
                    for copy in sends(d, m, h):
                        copy.wait_send()

        @pl.loop(0, groups)
        def _(m, d=d, ref=ref):
            for h in range(2):
                store(d, m, h, ref).wait()


def shards(slabs, laterals, thickness, layer_sources, green_down, column_down, green_up, column_up):
    depth, sources, width = layer_sources.shape
    blocks, bsize = green_down.shape[1], green_down.shape[-1]
    kcount = blocks // (width // bsize)
    rows = sources // MB
    half = HB * bsize
    result = jax.ShapeDtypeStruct((1, sources, width), jnp.bfloat16)
    smem = pl.BlockSpec(memory_space=pltpu.SMEM)
    anywhere = pl.BlockSpec(memory_space=pl.ANY)
    layer_sources, green_down, column_down, green_up, column_up = (
        pltpu.with_memory_space_constraint(array, pltpu.HBM)
        for array in (layer_sources, green_down, column_down, green_up, column_up)
    )
    return pl.pallas_call(
        functools.partial(sweep, slabs, laterals, kcount),
        out_shape=(result, result),
        in_specs=[smem, anywhere, anywhere, smem, anywhere, smem],
        out_specs=(anywhere, anywhere),
        scratch_shapes=[
            pltpu.VMEM((depth, sources, width), jnp.bfloat16),
            pltpu.VMEM((2, blocks, bsize, bsize), jnp.bfloat16),
            pltpu.VMEM((2, sources, half), jnp.float32),
            pltpu.VMEM((2, MB, 4, rows, half), jnp.bfloat16),
            pltpu.VMEM((4 * HB, rows, bsize), jnp.bfloat16),
            pltpu.VMEM((2, 2, sources, half), jnp.bfloat16),
            pltpu.SemaphoreType.DMA((MB,)),
            pltpu.SemaphoreType.DMA((2,)),
            pltpu.SemaphoreType.DMA((2, MB, 4)),
            pltpu.SemaphoreType.DMA((2, MB, 4)),
            pltpu.SemaphoreType.DMA((2, MB, 2)),
        ],
        compiler_params=pltpu.CompilerParams(
            collective_id=0, has_side_effects=True, vmem_limit_bytes=12 << 20
        ),
    )(thickness, layer_sources, green_down, column_down, green_up, column_up)


def solution(mesh):
    return jax.shard_map(
        functools.partial(shards, mesh.shape["slab"], mesh.shape["cross"]),
        mesh=mesh,
        in_specs=(
            P("slab"),
            P("slab", None, "cross"),
            P("slab", "cross", None, None),
            P("slab", "cross"),
            P("slab", "cross", None, None),
            P("slab", "cross"),
        ),
        out_specs=(P("slab", None, "cross"), P("slab", None, "cross")),
        check_vma=False,
    )
```

```python
import functools

import jax
import jax.numpy as jnp
from jax import lax
from jax.experimental import pallas as pl
from jax.experimental.pallas import tpu as pltpu
from jax.sharding import PartitionSpec as P

HB = 4
MB = 4
ROW = 4
START = 4
MESH = pl.DeviceIdType.MESH


def sweep(
    slabs, laterals, kcount,
    thick_ref, layers_hbm, gdown_hbm, cdown_ref, gup_hbm, cup_ref, cdown_hbm, cup_hbm,
    down_hbm, up_hbm,
    layers, green, source, ext, near, out, far_green, far_column, far_source, far_out,
    layer_sem, green_sem, recv_sem, send_sem, store_sem, far_recv, far_send,
):
    depth, _, width = layers.shape
    groups, rows = ext.shape[1], ext.shape[3]
    bsize = green.shape[-1]
    per_dev = width // bsize
    half = HB * bsize
    slab = lax.axis_index("slab")
    cross = lax.axis_index("cross")
    right = lax.rem(cross + 1, laterals)
    left = lax.rem(cross + laterals - 1, laterals)
    last = slabs - 1
    at = lax.rem(cross, ROW)
    border = jnp.logical_or(at == 0, at == ROW - 1)
    hx = jnp.where(at == 0, 0, 1)
    across = left + hx * (right - left)
    dx = lax.rem(slab, 2)
    inner = slab + dx * (last - 2 * slab) >= START
    helps = jnp.logical_and(border, inner)

    def group_rows(m):
        return pl.ds(pl.multiple_of(m * rows, rows), rows)

    def layer_copy(m):
        part = group_rows(m)
        return pltpu.make_async_copy(
            layers_hbm.at[:, part, :], layers.at[:, part, :], layer_sem.at[m]
        )

    green_copies = [
        pltpu.make_async_copy(gdown_hbm.at[0], green.at[0], green_sem.at[0]),
        pltpu.make_async_copy(gup_hbm.at[0], green.at[1], green_sem.at[1]),
    ]
    for m in range(groups):
        layer_copy(m).start()
    for copy in green_copies:
        copy.start()

    barrier = pltpu.get_barrier_semaphore()
    for step, there in ((1, slab < last), (-1, slab > 0)):
        @pl.when(there)
        def _(step=step):
            for side in (left, cross, right):
                pl.semaphore_signal(
                    barrier, inc=1,
                    device_id={"slab": slab + step, "cross": side}, device_id_type=MESH,
                )
    @pl.when(helps)
    def _():
        pl.semaphore_signal(
            barrier, inc=1, device_id={"slab": slab, "cross": across}, device_id_type=MESH
        )
    pl.semaphore_wait(
        barrier,
        3 * ((slab < last).astype(jnp.int32) + (slab > 0).astype(jnp.int32))
        + helps.astype(jnp.int32),
    )

    def place(d):
        return slab + d * (last - 2 * slab)

    def even(d):
        return jnp.logical_and(lax.rem(place(d), 2) == 0, place(d) >= START)

    def remote(d, m, src, piece, side, slot):
        return pltpu.make_async_remote_copy(
            src_ref=src,
            dst_ref=ext.at[d, m, piece],
            send_sem=send_sem.at[d, m, slot],
            recv_sem=recv_sem.at[d, m, piece],
            device_id={"slab": slab + 1 - 2 * d, "cross": side},
            device_id_type=MESH,
        )

    def own_half(d, m, h):
        return out.at[d, h, group_rows(m), :]

    def sends(d, m, h, act):
        crossing = jnp.logical_and(border, h == hx)

        @pl.when(jnp.logical_not(jnp.logical_and(crossing, even(d))))
        def _():
            act(remote(d, m, own_half(d, m, h), 3 - 3 * h, left + h * (right - left), 3 - 3 * h))
        act(remote(d, m, own_half(d, m, h), 1 + h, cross, 1 + h))

        @pl.when(
            jnp.logical_and(
                jnp.logical_and(border, h != hx),
                jnp.logical_and(lax.rem(place(d), 2) == 1, place(d) >= START - 1),
            )
        )
        def _():
            act(remote(d, m, own_half(d, m, h), 4, across, 4))

    def far_send_out(d, m, act):
        act(remote(d, m, far_out.at[m], 3 * hx, cross, 5))

    def over(src, dst, i):
        return pltpu.make_async_remote_copy(
            src_ref=src, dst_ref=dst, send_sem=far_send.at[i], recv_sem=far_recv.at[i],
            device_id={"slab": slab, "cross": across}, device_id_type=MESH,
        )

    per_half = HB * kcount

    def over_green(ref):
        return over(ref.at[0, pl.ds(hx * per_half, per_half)], far_green, 0)

    def over_source(m):
        return over(source.at[hx, group_rows(m), :], far_source.at[group_rows(m), :], 2 + m)

    def hand_over_green():
        for want, gref, cref in ((0, gdown_hbm, cdown_hbm), (1, gup_hbm, cup_hbm)):
            @pl.when(dx == want)
            def _(gref=gref, cref=cref):
                over(cref, far_column, 1).start()
                over_green(gref).start()

    def arrived(d, m, piece):
        remote(d, m, own_half(d, m, 0), piece, cross, piece).wait_recv()

    def has_send(d):
        return slab != last * (1 - d)

    def store(d, m, h, ref):
        return pltpu.make_async_copy(
            out.at[d, h, group_rows(m), :],
            ref.at[0, group_rows(m), h * half:(h + 1) * half],
            store_sem.at[d, m, h],
        )

    def emit(d, m, h):
        @pl.when(has_send(d))
        def _():
            sends(d, m, h, lambda copy: copy.start())

    def keep(d, m):
        for want, ref in ((0, down_hbm), (1, up_hbm)):
            @pl.when(d == want)
            def _(want=want, ref=ref):
                for h in range(2):
                    store(want, m, h, ref).start()

    first = jnp.where(slab < slabs // 2, 0, 1)
    edge = jnp.logical_or(slab == 0, slab == last)
    lead = jnp.where(at == 0, 1, 0)
    middle = jnp.logical_or(slab == slabs // 2, slab == slabs // 2 - 1)
    soon = jnp.logical_or(dx == first, middle)

    @pl.when(jnp.logical_and(helps, soon))
    def _():
        hand_over_green()

    @pl.loop(0, groups)
    def _(m):
        layer_copy(m).wait()
        part = group_rows(m)
        for h in range(2):
            total = None
            for k in range(depth):
                weight = (k < thick_ref[0]).astype(jnp.float32)
                term = layers[k, part, h * half:(h + 1) * half].astype(jnp.float32) * weight
                total = term if total is None else total + term
            source[h, part, :] = total

            @pl.when(edge)
            def _():
                out[first, h, part, :] = total.astype(out.dtype)
                emit(first, m, h)

        @pl.when(edge)
        def _():
            keep(first, m)

        @pl.when(jnp.logical_and(helps, soon))
        def _():
            over_source(m).start()

    for copy in green_copies:
        copy.wait()

    def flip(d):
        @pl.loop(0, green.shape[1], step=2)
        def _(i):
            for j in range(2):
                green[d, i + j] = green[d, i + j].T

    early = jnp.logical_and(slab >= slabs // 4, slab < slabs - slabs // 4)

    @pl.when(jnp.logical_not(edge))
    def _():
        flip(first)

    @pl.when(jnp.logical_or(early, edge))
    def _():
        flip(1 - first)

    def slot_of(raw):
        return jnp.bitwise_and(raw - cross * per_dev + 3 * HB, near.shape[0] - 1)

    def column(d, n):
        return slot_of(jnp.where(d == 0, cdown_ref[0, n], cup_ref[0, n]))

    def bring(d, m, piece, base):
        arrived(d, m, piece)
        for j in range(HB):
            near[base + j] = ext[d, m, piece, :, j * bsize:(j + 1) * bsize]

    @pl.loop(jnp.where(edge, groups, 0), 2 * groups)
    def _(t):
        later = t // groups
        m = t - later * groups
        d = first + later - 2 * first * later
        part = group_rows(m)

        @pl.when(jnp.logical_and(t == groups, jnp.logical_not(jnp.logical_or(early, edge))))
        def _():
            flip(d)

        @pl.when(
            jnp.logical_and(
                t == groups, jnp.logical_and(helps, jnp.logical_not(soon))
            )
        )
        def _():
            hand_over_green()
            for j in range(groups):
                over_source(j).start()

        @pl.loop(0, 2)
        def _(i):
            h = lead + i - 2 * lead * i

            @pl.when(i == 0)
            def _():
                bring(d, m, 1, 3 * HB)
                bring(d, m, 2, 4 * HB)

            bring(d, m, 3 * h, (2 + 3 * h) * HB)

            for b in range(HB):
                base = (h * HB + b) * kcount
                picked = jnp.concatenate(
                    [near[column(d, base + k)] for k in range(kcount)], axis=1
                )
                weights = green[d, pl.ds(base, kcount)].reshape(kcount * bsize, bsize)
                product = jnp.dot(picked, weights, preferred_element_type=jnp.float32)
                lanes = slice(b * bsize, (b + 1) * bsize)
                out[d, h, part, lanes] = (product + source[h, part, lanes]).astype(out.dtype)
            emit(d, m, h)

        @pl.when(jnp.logical_and(border, even(d)))
        def _():
            @pl.when(m == 0)
            def _():
                over(cdown_hbm, far_column, 1).wait_recv()
                over_green(gdown_hbm).wait_recv()
            over_source(m).wait_recv()
            bring(d, m, 4, (1 + 5 * hx) * HB)
            for b in range(HB):
                base = b * kcount
                picked = jnp.concatenate(
                    [
                        near[slot_of(far_column[0, (1 - hx) * per_half + base + k])]
                        for k in range(kcount)
                    ],
                    axis=1,
                )
                weights = jnp.concatenate([far_green[base + k] for k in range(kcount)], axis=1)
                product = lax.dot_general(
                    picked, weights, (((1,), (1,)), ((), ())),
                    preferred_element_type=jnp.float32,
                )
                lanes = slice(b * bsize, (b + 1) * bsize)
                far_out[m, :, lanes] = (product + far_source[part, lanes]).astype(far_out.dtype)
            far_send_out(d, m, lambda copy: copy.start())

        keep(d, m)

    @pl.when(helps)
    def _():
        over(cdown_hbm, far_column, 1).wait_send()
        over_green(gdown_hbm).wait_send()
        for j in range(groups):
            over_source(j).wait_send()

    for d, ref in ((0, down_hbm), (1, up_hbm)):
        @pl.when(has_send(d))
        def _(d=d):
            @pl.loop(0, groups)
            def _(m):
                for h in range(2):
                    sends(d, m, h, lambda copy: copy.wait_send())

                @pl.when(jnp.logical_and(border, even(d)))
                def _():
                    far_send_out(d, m, lambda copy: copy.wait_send())

        @pl.loop(0, groups)
        def _(m, d=d, ref=ref):
            for h in range(2):
                store(d, m, h, ref).wait()


def shards(slabs, laterals, thickness, layer_sources, green_down, column_down, green_up, column_up):
    depth, sources, width = layer_sources.shape
    blocks, bsize = green_down.shape[1], green_down.shape[-1]
    kcount = blocks // (width // bsize)
    rows = sources // MB
    half = HB * bsize
    result = jax.ShapeDtypeStruct((1, sources, width), jnp.bfloat16)
    smem = pl.BlockSpec(memory_space=pltpu.SMEM)
    anywhere = pl.BlockSpec(memory_space=pl.ANY)
    layer_sources, green_down, column_down, green_up, column_up = (
        pltpu.with_memory_space_constraint(array, pltpu.HBM)
        for array in (layer_sources, green_down, column_down, green_up, column_up)
    )
    return pl.pallas_call(
        functools.partial(sweep, slabs, laterals, kcount),
        out_shape=(result, result),
        in_specs=[smem, anywhere, anywhere, smem, anywhere, smem, anywhere, anywhere],
        out_specs=(anywhere, anywhere),
        scratch_shapes=[
            pltpu.VMEM((depth, sources, width), jnp.bfloat16),
            pltpu.VMEM((2, blocks, bsize, bsize), jnp.bfloat16),
            pltpu.VMEM((2, sources, half), jnp.float32),
            pltpu.VMEM((2, MB, 5, rows, half), jnp.bfloat16),
            pltpu.VMEM((8 * HB, rows, bsize), jnp.bfloat16),
            pltpu.VMEM((2, 2, sources, half), jnp.bfloat16),
            pltpu.VMEM((HB * kcount, bsize, bsize), jnp.bfloat16),
            pltpu.SMEM((1, blocks), jnp.int32),
            pltpu.VMEM((sources, half), jnp.float32),
            pltpu.VMEM((MB, rows, half), jnp.bfloat16),
            pltpu.SemaphoreType.DMA((MB,)),
            pltpu.SemaphoreType.DMA((2,)),
            pltpu.SemaphoreType.DMA((2, MB, 5)),
            pltpu.SemaphoreType.DMA((2, MB, 6)),
            pltpu.SemaphoreType.DMA((2, MB, 2)),
            pltpu.SemaphoreType.DMA((2 + MB,)),
            pltpu.SemaphoreType.DMA((2 + MB,)),
        ],
        compiler_params=pltpu.CompilerParams(
            collective_id=0, has_side_effects=True, vmem_limit_bytes=12 << 20
        ),
    )(
        thickness, layer_sources, green_down, column_down, green_up, column_up,
        column_down, column_up,
    )


def solution(mesh):
    return jax.shard_map(
        functools.partial(shards, mesh.shape["slab"], mesh.shape["cross"]),
        mesh=mesh,
        in_specs=(
            P("slab"),
            P("slab", None, "cross"),
            P("slab", "cross", None, None),
            P("slab", "cross"),
            P("slab", "cross", None, None),
            P("slab", "cross"),
        ),
        out_specs=(P("slab", None, "cross"), P("slab", None, "cross")),
        check_vma=False,
    )
```

```python
import functools

import jax
import jax.numpy as jnp
from jax import lax
from jax.experimental import pallas as pl
from jax.experimental.pallas import tpu as pltpu
from jax.sharding import PartitionSpec as P

HB = 4
MB = 8
ROW = 4
START = 4
MESH = pl.DeviceIdType.MESH


def sweep(
    slabs, laterals, kcount,
    thick_hbm, layers_hbm, gdown_hbm, cdown_hbm, gup_hbm, cup_hbm,
    down_hbm, up_hbm,
    thick_ref, cdown_ref, cup_ref, layers, green, source, ext, near, out, far_green, far_column, far_source, far_out,
    layer_sem, green_sem, recv_sem, send_sem, store_sem, far_recv, far_send, small_sem,
):
    depth, _, width = layers.shape
    groups, rows = ext.shape[1], ext.shape[3]
    bsize = green.shape[-1]
    per_dev = width // bsize
    half = HB * bsize
    slab = lax.axis_index("slab")
    cross = lax.axis_index("cross")
    right = lax.rem(cross + 1, laterals)
    left = lax.rem(cross + laterals - 1, laterals)
    last = slabs - 1
    at = lax.rem(cross, ROW)
    border = jnp.logical_or(at == 0, at == ROW - 1)
    hx = jnp.where(at == 0, 0, 1)
    across = left + hx * (right - left)
    dx = lax.rem(slab, 2)
    inner = slab + dx * (last - 2 * slab) >= START
    helps = jnp.logical_and(border, inner)

    def group_rows(m):
        return pl.ds(pl.multiple_of(m * rows, rows), rows)

    def layer_copy(m):
        part = group_rows(m)
        return pltpu.make_async_copy(
            layers_hbm.at[:, part, :], layers.at[:, part, :], layer_sem.at[m]
        )

    green_copies = [
        pltpu.make_async_copy(gdown_hbm.at[0], green.at[0], green_sem.at[0]),
        pltpu.make_async_copy(gup_hbm.at[0], green.at[1], green_sem.at[1]),
    ]
    thick_copy = pltpu.make_async_copy(thick_hbm, thick_ref, small_sem.at[0])
    column_copies = [
        pltpu.make_async_copy(cdown_hbm, cdown_ref, small_sem.at[1]),
        pltpu.make_async_copy(cup_hbm, cup_ref, small_sem.at[2]),
    ]
    thick_copy.start()
    for m in range(groups):
        layer_copy(m).start()
    for copy in column_copies:
        copy.start()
    for copy in green_copies:
        copy.start()

    barrier = pltpu.get_barrier_semaphore()
    for step, there in ((1, slab < last), (-1, slab > 0)):
        @pl.when(there)
        def _(step=step):
            for side in (left, cross, right):
                pl.semaphore_signal(
                    barrier, inc=1,
                    device_id={"slab": slab + step, "cross": side}, device_id_type=MESH,
                )
    @pl.when(helps)
    def _():
        pl.semaphore_signal(
            barrier, inc=1, device_id={"slab": slab, "cross": across}, device_id_type=MESH
        )
    pl.semaphore_wait(
        barrier,
        3 * ((slab < last).astype(jnp.int32) + (slab > 0).astype(jnp.int32))
        + helps.astype(jnp.int32),
    )

    def place(d):
        return slab + d * (last - 2 * slab)

    def even(d):
        return jnp.logical_and(lax.rem(place(d), 2) == 0, place(d) >= START)

    def remote(d, m, src, piece, side, slot):
        return pltpu.make_async_remote_copy(
            src_ref=src,
            dst_ref=ext.at[d, m, piece],
            send_sem=send_sem.at[d, m, slot],
            recv_sem=recv_sem.at[d, m, piece],
            device_id={"slab": slab + 1 - 2 * d, "cross": side},
            device_id_type=MESH,
        )

    def own_half(d, m, h):
        return out.at[d, h, group_rows(m), :]

    def sends(d, m, h, act):
        crossing = jnp.logical_and(border, h == hx)

        @pl.when(jnp.logical_not(jnp.logical_and(crossing, even(d))))
        def _():
            act(remote(d, m, own_half(d, m, h), 3 - 3 * h, left + h * (right - left), 3 - 3 * h))
        act(remote(d, m, own_half(d, m, h), 1 + h, cross, 1 + h))

        @pl.when(
            jnp.logical_and(
                jnp.logical_and(border, h != hx),
                jnp.logical_and(lax.rem(place(d), 2) == 1, place(d) >= START - 1),
            )
        )
        def _():
            act(remote(d, m, own_half(d, m, h), 4, across, 4))

    def far_send_out(d, m, act):
        act(remote(d, m, far_out.at[m], 3 * hx, cross, 5))

    def over(src, dst, i):
        return pltpu.make_async_remote_copy(
            src_ref=src, dst_ref=dst, send_sem=far_send.at[i], recv_sem=far_recv.at[i],
            device_id={"slab": slab, "cross": across}, device_id_type=MESH,
        )

    per_half = HB * kcount

    def over_green(ref):
        return over(ref.at[0, pl.ds(hx * per_half, per_half)], far_green, 0)

    def over_source(m):
        return over(source.at[hx, group_rows(m), :], far_source.at[group_rows(m), :], 2 + m)

    def hand_over_green():
        for want, gref, cref in ((0, gdown_hbm, cdown_hbm), (1, gup_hbm, cup_hbm)):
            @pl.when(dx == want)
            def _(gref=gref, cref=cref):
                over(cref, far_column, 1).start()
                over_green(gref).start()

    def arrived(d, m, piece):
        remote(d, m, own_half(d, m, 0), piece, cross, piece).wait_recv()

    def has_send(d):
        return slab != last * (1 - d)

    def store(d, m, h, ref):
        return pltpu.make_async_copy(
            out.at[d, h, group_rows(m), :],
            ref.at[0, group_rows(m), h * half:(h + 1) * half],
            store_sem.at[d, m, h],
        )

    def emit(d, m, h):
        @pl.when(has_send(d))
        def _():
            sends(d, m, h, lambda copy: copy.start())

    def keep(d, m):
        for want, ref in ((0, down_hbm), (1, up_hbm)):
            @pl.when(d == want)
            def _(want=want, ref=ref):
                for h in range(2):
                    store(want, m, h, ref).start()

    first = jnp.where(slab < slabs // 2, 0, 1)
    edge = jnp.logical_or(slab == 0, slab == last)
    lead = jnp.where(at == 0, 1, 0)
    middle = jnp.logical_or(slab == slabs // 2, slab == slabs // 2 - 1)
    soon = jnp.logical_or(dx == first, middle)

    @pl.when(jnp.logical_and(helps, soon))
    def _():
        hand_over_green()

    thick_copy.wait()

    @pl.loop(0, groups)
    def _(m):
        layer_copy(m).wait()
        part = group_rows(m)
        for h in range(2):
            total = None
            for k in range(depth):
                weight = (k < thick_ref[0]).astype(jnp.float32)
                term = layers[k, part, h * half:(h + 1) * half].astype(jnp.float32) * weight
                total = term if total is None else total + term
            source[h, part, :] = total

            @pl.when(edge)
            def _():
                out[first, h, part, :] = total.astype(out.dtype)
                emit(first, m, h)

        @pl.when(edge)
        def _():
            keep(first, m)

        @pl.when(jnp.logical_and(helps, soon))
        def _():
            over_source(m).start()

    for copy in column_copies + green_copies:
        copy.wait()

    def flip(d):
        @pl.loop(0, green.shape[1], step=2)
        def _(i):
            for j in range(2):
                green[d, i + j] = green[d, i + j].T

    early = jnp.logical_and(slab >= slabs // 4, slab < slabs - slabs // 4)

    @pl.when(jnp.logical_not(edge))
    def _():
        flip(first)

    @pl.when(jnp.logical_or(early, edge))
    def _():
        flip(1 - first)

    def take_far_green():
        over(cdown_hbm, far_column, 1).wait_recv()
        over_green(gdown_hbm).wait_recv()

        @pl.loop(0, far_green.shape[0], step=2)
        def _(i):
            for j in range(2):
                far_green[i + j] = far_green[i + j].T

    @pl.when(jnp.logical_and(helps, soon))
    def _():
        take_far_green()

    def slot_of(raw):
        return jnp.bitwise_and(raw - cross * per_dev + 3 * HB, near.shape[0] - 1)

    def column(d, n):
        return slot_of(jnp.where(d == 0, cdown_ref[0, n], cup_ref[0, n]))

    def bring(d, m, piece, base):
        arrived(d, m, piece)
        for j in range(HB):
            near[base + j] = ext[d, m, piece, :, j * bsize:(j + 1) * bsize]

    @pl.loop(jnp.where(edge, groups, 0), 2 * groups)
    def _(t):
        later = t // groups
        m = t - later * groups
        d = first + later - 2 * first * later
        part = group_rows(m)

        @pl.when(jnp.logical_and(t == groups, jnp.logical_not(jnp.logical_or(early, edge))))
        def _():
            flip(d)

        @pl.when(
            jnp.logical_and(
                t == groups, jnp.logical_and(helps, jnp.logical_not(soon))
            )
        )
        def _():
            hand_over_green()
            for j in range(groups):
                over_source(j).start()
            take_far_green()

        @pl.loop(0, 2)
        def _(i):
            h = lead + i - 2 * lead * i

            @pl.when(i == 0)
            def _():
                bring(d, m, 1, 3 * HB)
                bring(d, m, 2, 4 * HB)

            bring(d, m, 3 * h, (2 + 3 * h) * HB)

            for b in range(HB):
                base = (h * HB + b) * kcount
                picked = jnp.concatenate(
                    [near[column(d, base + k)] for k in range(kcount)], axis=1
                )
                weights = green[d, pl.ds(base, kcount)].reshape(kcount * bsize, bsize)
                product = jnp.dot(picked, weights, preferred_element_type=jnp.float32)
                lanes = slice(b * bsize, (b + 1) * bsize)
                out[d, h, part, lanes] = (product + source[h, part, lanes]).astype(out.dtype)
            emit(d, m, h)

        @pl.when(jnp.logical_and(border, even(d)))
        def _():
            over_source(m).wait_recv()
            bring(d, m, 4, (1 + 5 * hx) * HB)
            for b in range(HB):
                base = b * kcount
                picked = jnp.concatenate(
                    [
                        near[slot_of(far_column[0, (1 - hx) * per_half + base + k])]
                        for k in range(kcount)
                    ],
                    axis=1,
                )
                weights = far_green[base:base + kcount].reshape(kcount * bsize, bsize)
                product = jnp.dot(picked, weights, preferred_element_type=jnp.float32)
                lanes = slice(b * bsize, (b + 1) * bsize)
                far_out[m, :, lanes] = (product + far_source[part, lanes]).astype(far_out.dtype)
            far_send_out(d, m, lambda copy: copy.start())

        keep(d, m)

    @pl.when(helps)
    def _():
        over(cdown_hbm, far_column, 1).wait_send()
        over_green(gdown_hbm).wait_send()
        for j in range(groups):
            over_source(j).wait_send()

    for d, ref in ((0, down_hbm), (1, up_hbm)):
        @pl.when(has_send(d))
        def _(d=d):
            @pl.loop(0, groups)
            def _(m):
                for h in range(2):
                    sends(d, m, h, lambda copy: copy.wait_send())

                @pl.when(jnp.logical_and(border, even(d)))
                def _():
                    far_send_out(d, m, lambda copy: copy.wait_send())

        @pl.loop(0, groups)
        def _(m, d=d, ref=ref):
            for h in range(2):
                store(d, m, h, ref).wait()


def put_out(down_ref, up_ref, down_out, up_out, sem):
    copies = [
        pltpu.make_async_copy(down_ref, down_out, sem.at[0]),
        pltpu.make_async_copy(up_ref, up_out, sem.at[1]),
    ]
    for copy in copies:
        copy.start()
    for copy in copies:
        copy.wait()


def shards(slabs, laterals, thickness, layer_sources, green_down, column_down, green_up, column_up):
    depth, sources, width = layer_sources.shape
    blocks, bsize = green_down.shape[1], green_down.shape[-1]
    kcount = blocks // (width // bsize)
    rows = sources // MB
    half = HB * bsize
    result = jax.ShapeDtypeStruct((1, sources, width), jnp.bfloat16)
    anywhere = pl.BlockSpec(memory_space=pl.ANY)
    given = (layer_sources, green_down, column_down, green_up, column_up)
    given = [pltpu.with_memory_space_constraint(array, pltpu.HBM) for array in given]
    traces = pl.pallas_call(
        functools.partial(sweep, slabs, laterals, kcount),
        out_shape=(result, result),
        in_specs=[anywhere] * 6,
        out_specs=(anywhere, anywhere),
        scratch_shapes=[
            pltpu.SMEM((1,), jnp.int32),
            pltpu.SMEM((1, blocks), jnp.int32),
            pltpu.SMEM((1, blocks), jnp.int32),
            pltpu.VMEM((depth, sources, width), jnp.bfloat16),
            pltpu.VMEM((2, blocks, bsize, bsize), jnp.bfloat16),
            pltpu.VMEM((2, sources, half), jnp.float32),
            pltpu.VMEM((2, MB, 5, rows, half), jnp.bfloat16),
            pltpu.VMEM((8 * HB, rows, bsize), jnp.bfloat16),
            pltpu.VMEM((2, 2, sources, half), jnp.bfloat16),
            pltpu.VMEM((HB * kcount, bsize, bsize), jnp.bfloat16),
            pltpu.SMEM((1, blocks), jnp.int32),
            pltpu.VMEM((sources, half), jnp.float32),
            pltpu.VMEM((MB, rows, half), jnp.bfloat16),
            pltpu.SemaphoreType.DMA((MB,)),
            pltpu.SemaphoreType.DMA((2,)),
            pltpu.SemaphoreType.DMA((2, MB, 5)),
            pltpu.SemaphoreType.DMA((2, MB, 6)),
            pltpu.SemaphoreType.DMA((2, MB, 2)),
            pltpu.SemaphoreType.DMA((2 + MB,)),
            pltpu.SemaphoreType.DMA((2 + MB,)),
            pltpu.SemaphoreType.DMA((3,)),
        ],
        compiler_params=pltpu.CompilerParams(
            collective_id=0, has_side_effects=True, vmem_limit_bytes=12 << 20
        ),
    )(thickness, *given)
    return pl.pallas_call(
        put_out,
        out_shape=(result, result),
        in_specs=[anywhere] * 2,
        out_specs=(anywhere, anywhere),
        scratch_shapes=[pltpu.SemaphoreType.DMA((2,))],
        compiler_params=pltpu.CompilerParams(vmem_limit_bytes=1 << 20),
    )(*traces)


def solution(mesh):
    return jax.shard_map(
        functools.partial(shards, mesh.shape["slab"], mesh.shape["cross"]),
        mesh=mesh,
        in_specs=(
            P("slab"),
            P("slab", None, "cross"),
            P("slab", "cross", None, None),
            P("slab", "cross"),
            P("slab", "cross", None, None),
            P("slab", "cross"),
        ),
        out_specs=(P("slab", None, "cross"), P("slab", None, "cross")),
        check_vma=False,
    )
```

```python
import functools

import jax
import jax.numpy as jnp
from jax import lax
from jax.experimental import pallas as pl
from jax.experimental.pallas import tpu as pltpu
from jax.sharding import PartitionSpec as P

HB = 4
MB = 8
ROW = 4
START = 4
MESH = pl.DeviceIdType.MESH


def sweep(
    slabs, laterals, kcount,
    thick_hbm, layers_hbm, gdown_hbm, cdown_hbm, gup_hbm, cup_hbm,
    down_hbm, up_hbm,
    thick_ref, cdown_ref, cup_ref, layers, green, source, ext, near, out, far_green, far_column, far_source, far_out,
    layer_sem, green_sem, recv_sem, send_sem, store_sem, far_recv, far_send, small_sem,
):
    depth, _, width = layers.shape
    groups, rows = ext.shape[1], ext.shape[3]
    bsize = green.shape[-1]
    per_dev = width // bsize
    half = HB * bsize
    slab = lax.axis_index("slab")
    cross = lax.axis_index("cross")
    right = lax.rem(cross + 1, laterals)
    left = lax.rem(cross + laterals - 1, laterals)
    last = slabs - 1
    at = lax.rem(cross, ROW)
    border = jnp.logical_or(at == 0, at == ROW - 1)
    hx = jnp.where(at == 0, 0, 1)
    across = left + hx * (right - left)
    dx = lax.rem(slab, 2)
    inner = slab + dx * (last - 2 * slab) >= START
    helps = jnp.logical_and(border, inner)

    def group_rows(m):
        return pl.ds(pl.multiple_of(m * rows, rows), rows)

    def layer_copy(m):
        part = group_rows(m)
        return pltpu.make_async_copy(
            layers_hbm.at[:, part, :], layers.at[:, part, :], layer_sem.at[m]
        )

    green_copies = [
        pltpu.make_async_copy(gdown_hbm.at[0], green.at[0], green_sem.at[0]),
        pltpu.make_async_copy(gup_hbm.at[0], green.at[1], green_sem.at[1]),
    ]
    thick_copy = pltpu.make_async_copy(thick_hbm, thick_ref, small_sem.at[0])
    column_copies = [
        pltpu.make_async_copy(cdown_hbm, cdown_ref, small_sem.at[1]),
        pltpu.make_async_copy(cup_hbm, cup_ref, small_sem.at[2]),
    ]
    thick_copy.start()
    for m in range(groups):
        layer_copy(m).start()
    for copy in column_copies:
        copy.start()
    for copy in green_copies:
        copy.start()

    barrier = pltpu.get_barrier_semaphore()
    for step, there in ((1, slab < last), (-1, slab > 0)):
        @pl.when(there)
        def _(step=step):
            for side in (left, cross, right):
                pl.semaphore_signal(
                    barrier, inc=1,
                    device_id={"slab": slab + step, "cross": side}, device_id_type=MESH,
                )
    @pl.when(helps)
    def _():
        pl.semaphore_signal(
            barrier, inc=1, device_id={"slab": slab, "cross": across}, device_id_type=MESH
        )
    pl.semaphore_wait(
        barrier,
        3 * ((slab < last).astype(jnp.int32) + (slab > 0).astype(jnp.int32))
        + helps.astype(jnp.int32),
    )

    def place(d):
        return slab + d * (last - 2 * slab)

    def even(d):
        return jnp.logical_and(lax.rem(place(d), 2) == 0, place(d) >= START)

    def remote(d, m, src, piece, side, slot):
        return pltpu.make_async_remote_copy(
            src_ref=src,
            dst_ref=ext.at[d, m, piece],
            send_sem=send_sem.at[d, m, slot],
            recv_sem=recv_sem.at[d, m, piece],
            device_id={"slab": slab + 1 - 2 * d, "cross": side},
            device_id_type=MESH,
        )

    def own_half(d, m, h):
        return out.at[d, h, group_rows(m), :]

    def sends(d, m, h, act):
        crossing = jnp.logical_and(border, h == hx)

        @pl.when(jnp.logical_not(jnp.logical_and(crossing, even(d))))
        def _():
            act(remote(d, m, own_half(d, m, h), 3 - 3 * h, left + h * (right - left), 3 - 3 * h))
        act(remote(d, m, own_half(d, m, h), 1 + h, cross, 1 + h))

        @pl.when(
            jnp.logical_and(
                jnp.logical_and(border, h != hx),
                jnp.logical_and(lax.rem(place(d), 2) == 1, place(d) >= START - 1),
            )
        )
        def _():
            act(remote(d, m, own_half(d, m, h), 4, across, 4))

    def far_send_out(d, m, act):
        act(remote(d, m, far_out.at[m], 3 * hx, cross, 5))

    def over(src, dst, i):
        return pltpu.make_async_remote_copy(
            src_ref=src, dst_ref=dst, send_sem=far_send.at[i], recv_sem=far_recv.at[i],
            device_id={"slab": slab, "cross": across}, device_id_type=MESH,
        )

    per_half = HB * kcount

    def over_green(ref):
        return over(ref.at[0, pl.ds(hx * per_half, per_half)], far_green, 0)

    def over_source(m):
        return over(source.at[hx, group_rows(m), :], far_source.at[group_rows(m), :], 2 + m)

    def hand_over_green():
        for want, gref, cref in ((0, gdown_hbm, cdown_hbm), (1, gup_hbm, cup_hbm)):
            @pl.when(dx == want)
            def _(gref=gref, cref=cref):
                over(cref, far_column, 1).start()
                over_green(gref).start()

    def arrived(d, m, piece):
        remote(d, m, own_half(d, m, 0), piece, cross, piece).wait_recv()

    def has_send(d):
        return slab != last * (1 - d)

    def store(d, m, h, ref):
        return pltpu.make_async_copy(
            out.at[d, h, group_rows(m), :],
            ref.at[0, group_rows(m), h * half:(h + 1) * half],
            store_sem.at[d, m, h],
        )

    def emit(d, m, h):
        @pl.when(has_send(d))
        def _():
            sends(d, m, h, lambda copy: copy.start())

    def keep(d, m):
        for want, ref in ((0, down_hbm), (1, up_hbm)):
            @pl.when(d == want)
            def _(want=want, ref=ref):
                for h in range(2):
                    store(want, m, h, ref).start()

    first = jnp.where(slab < slabs // 2, 0, 1)
    edge = jnp.logical_or(slab == 0, slab == last)
    lead = jnp.where(at == 0, 1, 0)
    middle = jnp.logical_or(slab == slabs // 2, slab == slabs // 2 - 1)
    soon = jnp.logical_or(dx == first, middle)

    @pl.when(jnp.logical_and(helps, soon))
    def _():
        hand_over_green()

    thick_copy.wait()

    @pl.loop(0, groups)
    def _(m):
        layer_copy(m).wait()
        part = group_rows(m)
        for h in range(2):
            total = None
            for k in range(depth):
                weight = (k < thick_ref[0]).astype(jnp.float32)
                term = layers[k, part, h * half:(h + 1) * half].astype(jnp.float32) * weight
                total = term if total is None else total + term
            source[h, part, :] = total

            @pl.when(edge)
            def _():
                out[first, h, part, :] = total.astype(out.dtype)
                emit(first, m, h)

        @pl.when(edge)
        def _():
            keep(first, m)

        @pl.when(jnp.logical_and(helps, soon))
        def _():
            over_source(m).start()

    for copy in column_copies + green_copies:
        copy.wait()

    def flip(d):
        @pl.loop(0, green.shape[1], step=2)
        def _(i):
            for j in range(2):
                green[d, i + j] = green[d, i + j].T

    early = jnp.logical_and(slab >= slabs // 4, slab < slabs - slabs // 4)

    @pl.when(jnp.logical_not(edge))
    def _():
        flip(first)

    @pl.when(jnp.logical_or(early, edge))
    def _():
        flip(1 - first)

    def take_far_green():
        over(cdown_hbm, far_column, 1).wait_recv()
        over_green(gdown_hbm).wait_recv()

        @pl.loop(0, far_green.shape[0], step=2)
        def _(i):
            for j in range(2):
                far_green[i + j] = far_green[i + j].T

    @pl.when(jnp.logical_and(helps, soon))
    def _():
        take_far_green()

    def slot_of(raw):
        return jnp.bitwise_and(raw - cross * per_dev + 3 * HB, near.shape[0] - 1)

    def column(d, n):
        return slot_of(jnp.where(d == 0, cdown_ref[0, n], cup_ref[0, n]))

    def bring(d, m, piece, base):
        arrived(d, m, piece)
        for j in range(HB):
            near[base + j] = ext[d, m, piece, :, j * bsize:(j + 1) * bsize]

    @pl.loop(jnp.where(edge, groups, 0), 2 * groups)
    def _(t):
        later = t // groups
        m = t - later * groups
        d = first + later - 2 * first * later
        part = group_rows(m)

        @pl.when(jnp.logical_and(t == groups, jnp.logical_not(jnp.logical_or(early, edge))))
        def _():
            flip(d)

        @pl.when(
            jnp.logical_and(
                t == groups, jnp.logical_and(helps, jnp.logical_not(soon))
            )
        )
        def _():
            hand_over_green()
            for j in range(groups):
                over_source(j).start()
            take_far_green()

        @pl.loop(0, 2, unroll=True)
        def _(i):
            h = lead + i - 2 * lead * i

            @pl.when(i == 0)
            def _():
                bring(d, m, 1, 3 * HB)
                bring(d, m, 2, 4 * HB)

            bring(d, m, 3 * h, (2 + 3 * h) * HB)

            for b in range(HB):
                base = (h * HB + b) * kcount
                picked = jnp.concatenate(
                    [near[column(d, base + k)] for k in range(kcount)], axis=1
                )
                weights = green[d, pl.ds(base, kcount)].reshape(kcount * bsize, bsize)
                product = jnp.dot(picked, weights, preferred_element_type=jnp.float32)
                lanes = slice(b * bsize, (b + 1) * bsize)
                out[d, h, part, lanes] = (product + source[h, part, lanes]).astype(out.dtype)
            emit(d, m, h)

        @pl.when(jnp.logical_and(border, even(d)))
        def _():
            over_source(m).wait_recv()
            bring(d, m, 4, (1 + 5 * hx) * HB)
            for b in range(HB):
                base = b * kcount
                picked = jnp.concatenate(
                    [
                        near[slot_of(far_column[0, (1 - hx) * per_half + base + k])]
                        for k in range(kcount)
                    ],
                    axis=1,
                )
                weights = far_green[base:base + kcount].reshape(kcount * bsize, bsize)
                product = jnp.dot(picked, weights, preferred_element_type=jnp.float32)
                lanes = slice(b * bsize, (b + 1) * bsize)
                far_out[m, :, lanes] = (product + far_source[part, lanes]).astype(far_out.dtype)
            far_send_out(d, m, lambda copy: copy.start())

        keep(d, m)

    @pl.when(helps)
    def _():
        over(cdown_hbm, far_column, 1).wait_send()
        over_green(gdown_hbm).wait_send()
        for j in range(groups):
            over_source(j).wait_send()

    for d, ref in ((0, down_hbm), (1, up_hbm)):
        @pl.when(has_send(d))
        def _(d=d):
            @pl.loop(0, groups)
            def _(m):
                for h in range(2):
                    sends(d, m, h, lambda copy: copy.wait_send())

                @pl.when(jnp.logical_and(border, even(d)))
                def _():
                    far_send_out(d, m, lambda copy: copy.wait_send())

        @pl.loop(0, groups)
        def _(m, d=d, ref=ref):
            for h in range(2):
                store(d, m, h, ref).wait()


def put_out(down_ref, up_ref, down_out, up_out, sem):
    copies = [
        pltpu.make_async_copy(down_ref, down_out, sem.at[0]),
        pltpu.make_async_copy(up_ref, up_out, sem.at[1]),
    ]
    for copy in copies:
        copy.start()
    for copy in copies:
        copy.wait()


def shards(slabs, laterals, thickness, layer_sources, green_down, column_down, green_up, column_up):
    depth, sources, width = layer_sources.shape
    blocks, bsize = green_down.shape[1], green_down.shape[-1]
    kcount = blocks // (width // bsize)
    rows = sources // MB
    half = HB * bsize
    result = jax.ShapeDtypeStruct((1, sources, width), jnp.bfloat16)
    anywhere = pl.BlockSpec(memory_space=pl.ANY)
    given = (layer_sources, green_down, column_down, green_up, column_up)
    given = [pltpu.with_memory_space_constraint(array, pltpu.HBM) for array in given]
    traces = pl.pallas_call(
        functools.partial(sweep, slabs, laterals, kcount),
        out_shape=(result, result),
        in_specs=[anywhere] * 6,
        out_specs=(anywhere, anywhere),
        scratch_shapes=[
            pltpu.SMEM((1,), jnp.int32),
            pltpu.SMEM((1, blocks), jnp.int32),
            pltpu.SMEM((1, blocks), jnp.int32),
            pltpu.VMEM((depth, sources, width), jnp.bfloat16),
            pltpu.VMEM((2, blocks, bsize, bsize), jnp.bfloat16),
            pltpu.VMEM((2, sources, half), jnp.float32),
            pltpu.VMEM((2, MB, 5, rows, half), jnp.bfloat16),
            pltpu.VMEM((8 * HB, rows, bsize), jnp.bfloat16),
            pltpu.VMEM((2, 2, sources, half), jnp.bfloat16),
            pltpu.VMEM((HB * kcount, bsize, bsize), jnp.bfloat16),
            pltpu.SMEM((1, blocks), jnp.int32),
            pltpu.VMEM((sources, half), jnp.float32),
            pltpu.VMEM((MB, rows, half), jnp.bfloat16),
            pltpu.SemaphoreType.DMA((MB,)),
            pltpu.SemaphoreType.DMA((2,)),
            pltpu.SemaphoreType.DMA((2, MB, 5)),
            pltpu.SemaphoreType.DMA((2, MB, 6)),
            pltpu.SemaphoreType.DMA((2, MB, 2)),
            pltpu.SemaphoreType.DMA((2 + MB,)),
            pltpu.SemaphoreType.DMA((2 + MB,)),
            pltpu.SemaphoreType.DMA((3,)),
        ],
        compiler_params=pltpu.CompilerParams(
            collective_id=0, has_side_effects=True, vmem_limit_bytes=12 << 20
        ),
    )(thickness, *given)
    return pl.pallas_call(
        put_out,
        out_shape=(result, result),
        in_specs=[anywhere] * 2,
        out_specs=(anywhere, anywhere),
        scratch_shapes=[pltpu.SemaphoreType.DMA((2,))],
        compiler_params=pltpu.CompilerParams(vmem_limit_bytes=1 << 20),
    )(*traces)


def solution(mesh):
    return jax.shard_map(
        functools.partial(shards, mesh.shape["slab"], mesh.shape["cross"]),
        mesh=mesh,
        in_specs=(
            P("slab"),
            P("slab", None, "cross"),
            P("slab", "cross", None, None),
            P("slab", "cross"),
            P("slab", "cross", None, None),
            P("slab", "cross"),
        ),
        out_specs=(P("slab", None, "cross"), P("slab", None, "cross")),
        check_vma=False,
    )
```
